128 devices in a mesh: dp: 16 (over x, z_lo, core), tensor: 8 (over z_hi, y).
Axes of the slice: x: 4, y: 4, z: 4 (z_hi: 2, z_lo: 2; z = z_hi * 2 + z_lo), core: 2. Of those that a mesh axis runs over, the one named last changes fastest.
Arguments:
- inputs: bfloat16 [4096, 4096], P('dp', 'tensor'), may hold values from -6 to 6
- gate_pre: bfloat16 [4096, 14336], P('dp', 'tensor'), may hold values from -9 to 9
- up_pre: bfloat16 [4096, 14336], P('dp', 'tensor'), may hold values from -6 to 6
- out_grad: bfloat16 [4096, 4096], P('dp', 'tensor'), may hold values from -0.09375 to 0.09375
- down_weight: bfloat16 [14336, 4096], P('tensor'), may hold values from -0.09375 to 0.09375
Outputs:
- gate_wgrad: bfloat16 [4096, 14336], P('dp', 'tensor')
- up_wgrad: bfloat16 [4096, 14336], P('dp', 'tensor')
- in_cov: float32 [4096, 1024], P(('dp', 'tensor'))
- gate_cov: float32 [8, 1792, 896], P('tensor', 'dp')
- up_cov: float32 [8, 1792, 896], P('tensor', 'dp')
The draws below stay inside these ranges and needn't reach their ends.
All inputs are finite; a program needn't handle non-finite values.
Results may differ from the reference program's by a relative error of at most 0.014.
Values may be sent and summed in bfloat16 or wider, within the bound.
A program may use at most 192 MiB of HBM per device.

```python
import jax
import jax.numpy as jnp

D = 4096
FF = 14336
BLK = 1024
HBLK = 896
TOKENS = 4096
SHARDS = 8


def levels(rng, extent, cuts, least, largest):
    factor_of, own = 1.0, jax.random.fold_in(rng, 6)
    for axis_at, parts in cuts:
        draws = jnp.exp(jax.random.uniform(jax.random.fold_in(own, axis_at), (parts,), jnp.float32, least / len(cuts), largest / len(cuts)))
        factor_of = factor_of * jnp.repeat(draws, extent[axis_at] // parts).reshape([-1 if axis == axis_at else 1 for axis in range(len(extent))])
    return factor_of


def bell_draw(own_key, dims, width, limit, split=(), held_as=jnp.bfloat16):
    factor_of = levels(own_key, dims, split, -0.22, 0.18) if split else 1.0
    drawn = jax.random.normal(own_key, dims, jnp.float32) * width * factor_of
    return jnp.minimum(jnp.maximum(drawn, -limit), limit).astype(held_as)


def setup_inputs(seed: int = 0) -> dict:
    streams_of = jax.random.split(jax.random.key(seed), 6)
    inputs = bell_draw(streams_of[0], (TOKENS, D), 1.0, 6.0, ((0, 16), (1, 8)))
    gate_pre = bell_draw(streams_of[1], (TOKENS, FF), 1.5, 9.0, ((0, 16), (1, 8)))
    up_pre = bell_draw(streams_of[2], (TOKENS, FF), 1.0, 6.0, ((0, 16), (1, 8)))
    out_grad = bell_draw(streams_of[3], (TOKENS, D), (1.0 / TOKENS ** 0.5), 0.09375, ((0, 16), (1, 8)))
    down_weight = bell_draw(streams_of[4], (FF, D), D ** -0.5, 0.09375, ((0, 8),))
    return dict(inputs=inputs, gate_pre=gate_pre, up_pre=up_pre, out_grad=out_grad, down_weight=down_weight)


def reference(inputs, gate_pre, up_pre, out_grad, down_weight):
    hidden_grad = jnp.dot(out_grad, down_weight.T, preferred_element_type=jnp.float32)
    gate = gate_pre.astype(jnp.float32)
    up = up_pre.astype(jnp.float32)
    sig = jax.nn.sigmoid(gate)
    gate_grad = (hidden_grad * up * sig * (1.0 + gate * (1.0 - sig))).astype(jnp.bfloat16)
    up_grad = (hidden_grad * gate * sig).astype(jnp.bfloat16)
    gate_wgrad = jnp.dot(inputs.T, gate_grad, preferred_element_type=jnp.float32).astype(jnp.bfloat16)
    up_wgrad = jnp.dot(inputs.T, up_grad, preferred_element_type=jnp.float32).astype(jnp.bfloat16)
    tiled = inputs.astype(jnp.float32).reshape(TOKENS, D // BLK, BLK)
    in_cov = (jnp.einsum("tkb,tkc->kbc", tiled, tiled) / TOKENS).reshape(D, BLK)
    gate_tiles = gate_grad.astype(jnp.float32).reshape(TOKENS, FF // HBLK, HBLK)
    gate_cov = jnp.einsum("tkb,tkc->kbc", gate_tiles, gate_tiles).reshape(SHARDS, FF // SHARDS, HBLK)
    up_tiles = up_grad.astype(jnp.float32).reshape(TOKENS, FF // HBLK, HBLK)
    up_cov = jnp.einsum("tkb,tkc->kbc", up_tiles, up_tiles).reshape(SHARDS, FF // SHARDS, HBLK)
    return gate_wgrad, up_wgrad, in_cov, gate_cov, up_cov
```

```python
import jax
import jax.numpy as jnp
from jax import lax
from jax.experimental import pallas as pl
from jax.experimental.pallas import tpu as pltpu
from jax.sharding import PartitionSpec as P

MESH = pl.DeviceIdType.MESH
BF = jnp.bfloat16
F32 = jnp.float32

TOK = 256
NA = 64
NB = TOK - NA
D = 4096
DS = 512
H = 1792
CH = 128
CW = 2 * CH
NC = H // CH
BC = 7
HB = 896
T4 = 4 * TOK
DB = 1024
CR = 112
KSLOTS = 4


def kernel(
    x_hbm, gp_hbm, up_hbm, og_hbm, w_hbm,
    gw_ref, uw_ref, ic_ref, gc_ref, uc_ref,
    og, w, gp, up, g, xin, xt, ks, crv, fin, zs, zr, rt, cv, ccr, zcs, zcr, ic, icr, zis, zir,
    loc, wsem,
    oa_s, oa_r, ob_s, ob_r, xs_s, xs_r, xg_s, xg_r,
    a_s, a_r, af_s, af_r, b_s, b_r, bf_s, bf_r,
    k_s, k_r, z_s, z_r, m_s, m_r,
):
    dp = lax.axis_index("dp")
    t = lax.axis_index("tensor")
    x, zl, c = dp // 4, (dp // 2) % 2, dp % 2
    zh, y = t // 4, t % 4
    xp, xm, x2 = (x + 1) % 4, (x + 3) % 4, (x + 2) % 4
    yp, ym, y2 = (y + 1) % 4, (y + 3) % 4, (y + 2) % 4
    inplane = zl * 2 + c

    def at_x(v):
        return (v * 4 + inplane, t)

    def at_t(zz, yy):
        return (dp, zz * 4 + yy)

    mate = (dp + 1 - 2 * c, t)
    across = (dp + 2 - 4 * zl, t)
    zo = 1 - zh

    def rc(src, dst, ss, rs, dev):
        return pltpu.make_async_remote_copy(
            src_ref=src, dst_ref=dst, send_sem=ss, recv_sem=rs, device_id=dev, device_id_type=MESH
        )

    l_gp = pltpu.make_async_copy(gp_hbm, gp, loc.at[0])
    l_up = pltpu.make_async_copy(up_hbm, up, loc.at[1])
    own_cols = pl.ds(pl.multiple_of(t * DS, DS), DS)
    l_og = pltpu.make_async_copy(og_hbm, og.at[:, own_cols], loc.at[2])
    l_og.start()
    l_gp.start()
    l_up.start()

    def w_copy(j):
        r = pl.ds(pl.multiple_of(j * CH, CH), CH)
        return pltpu.make_async_copy(w_hbm.at[r, :], w.at[r, :], wsem.at[j])

    @pl.loop(0, NC)
    def _(j):
        w_copy(j).start()

    barrier = pltpu.get_barrier_semaphore()

    def here(dev):
        pl.semaphore_signal(barrier, inc=1, device_id=dev, device_id_type=MESH)

    for dz in range(2):
        for dy in range(4):
            if (dz, dy) != (0, 0):
                here(at_t((zh + dz) % 2, (y + dy) % 4))
    here(at_x(xp))
    here(at_x(xm))
    here(mate)
    here(across)
    xd = 2 * zh + y // 2
    half = y % 2
    self_x = xd == x
    for k in range(8):
        sx, sy, sz = k // 2, 2 * (x % 2) + k % 2, x // 2
        mine = jnp.logical_and(sx == x, jnp.logical_and(sy == y, sz == zh))

        @pl.when(jnp.logical_not(mine))
        def _():
            here((sx * 4 + inplane, sz * 4 + sy))

    pl.semaphore_wait(barrier, 19 - jnp.where(self_x, 1, 0))

    oa = []
    for dz in range(2):
        for dy in range(4):
            if (dz, dy) != (0, 0):
                cp = rc(
                    og_hbm.at[pl.ds(0, NA), :],
                    og.at[pl.ds(0, NA), own_cols],
                    oa_s.at[dz, dy],
                    oa_r.at[dz, dy],
                    at_t((zh + dz) % 2, (y + dy) % 4),
                )
                cp.start()
                oa.append(cp)

    half_cols = pl.ds(pl.multiple_of(half * DS, DS), DS)

    def scatter(k):
        return rc(
            x_hbm.at[pl.ds(k * 32, 32), :],
            xin.at[x, k, :, half_cols],
            xs_s.at[k],
            xs_r.at[x * 2 + half],
            (xd * 4 + inplane, k),
        )

    own_piece = pltpu.make_async_copy(
        x_hbm.at[pl.ds(pl.multiple_of(t * 32, 32), 32), :],
        xin.at[x, t, :, half_cols],
        xs_r.at[x * 2 + half],
    )
    for k in range(8):
        is_me = jnp.logical_and(self_x, t == k)

        @pl.when(is_me)
        def _():
            own_piece.start()

        @pl.when(jnp.logical_not(is_me))
        def _():
            scatter(k).start()

    def og_part(owner, part):
        cols = pl.ds(pl.multiple_of(owner * DS, DS), DS)
        rows = {0: pl.ds(NA, NB), 1: pl.ds(NA, NB // 2), 2: pl.ds(NA + NB // 2, NB // 2)}[part]
        return og.at[rows, cols]

    def x_part(owner, part):
        lead = {0: pl.ds(0, 4), 1: pl.ds(0, 2), 2: pl.ds(2, 2)}[part]
        return xin.at[lead, owner]

    def gather(part_of, first, ss, rs):
        def step(i):
            if i < 3:
                dev = (at_t(zo, y), at_t(zh, yp), at_t(zh, ym))[i]
                return rc(first, part_of(t, 0), ss.at[i], rs.at[i], dev)
            if i < 5:
                dev = (at_t(zh, yp), at_t(zh, ym))[i - 3]
                blk = part_of(zo * 4 + y, 0)
                return rc(blk, blk, ss.at[i], rs.at[i], dev)
            zz = (zh, zo)[(i - 5) // 2]
            if i % 2 == 1:
                blk = part_of(zz * 4 + ym, 1)
                return rc(blk, blk, ss.at[i], rs.at[i], at_t(zh, yp))
            blk = part_of(zz * 4 + yp, 2)
            return rc(blk, blk, ss.at[i], rs.at[i], at_t(zh, ym))

        def landed(i):
            where = (
                part_of(zo * 4 + y, 0), part_of(zh * 4 + ym, 0), part_of(zh * 4 + yp, 0),
                part_of(zo * 4 + ym, 0), part_of(zo * 4 + yp, 0),
                part_of(zh * 4 + y2, 1), part_of(zh * 4 + y2, 2),
                part_of(zo * 4 + y2, 1), part_of(zo * 4 + y2, 2),
            )[i]
            rc(where, where, ss.at[i], rs.at[i], at_t(zo, y)).wait_recv()

        return step, landed

    ob_step, ob_landed = gather(og_part, og_hbm.at[pl.ds(NA, NB), :], ob_s, ob_r)
    xg_step, xg_landed = gather(x_part, x_part(t, 0), xg_s, xg_r)
    for i in range(3):
        ob_step(i).start()

    for k in range(8):
        sx, sh = k // 2, k % 2
        dst = xin.at[sx, t, :, pl.ds(sh * DS, DS)]
        rc(dst, dst, xs_s.at[0], xs_r.at[k], mate).wait_recv()
    for i in range(3):
        xg_step(i).start()

    l_og.wait()
    l_gp.wait()
    l_up.wait()
    for dz in range(2):
        for dy in range(4):
            if (dz, dy) != (0, 0):
                oc = ((zh + 2 - dz) % 2) * 4 + (y + 4 - dy) % 4
                dst = og.at[pl.ds(0, NA), pl.ds(pl.multiple_of(oc * DS, DS), DS)]
                rc(dst, dst, oa_s.at[dz, dy], oa_r.at[dz, dy], mate).wait_recv()

    def grads(j, r0, n):
        hid = pl.ds(pl.multiple_of(j * CH, CH), CH)
        hg = lax.dot_general(
            og[pl.ds(r0, n), :], w[hid, :], (((1,), (1,)), ((), ())), preferred_element_type=F32
        )
        gate = gp[pl.ds(r0, n), hid].astype(F32)
        upv = up[pl.ds(r0, n), hid].astype(F32)
        sig = jax.nn.sigmoid(gate)
        hs = hg * sig
        rows = pl.ds(pl.multiple_of(x * TOK + r0, 16), n)
        g[j, rows, pl.ds(0, CH)] = (hs * upv * (1.0 + gate * (1.0 - sig))).astype(BF)
        g[j, rows, pl.ds(CH, CH)] = (hs * gate).astype(BF)

    def xrows(xx, r0, n):
        return pl.ds(pl.multiple_of(xx * TOK + r0, 16), n)

    def ring(r0, n, s_s, s_r, f_s, f_r):
        h = n // 2

        def send(j, way):
            blk = g.at[j, xrows(x, r0, n), :]
            return rc(blk, blk, s_s.at[j, way], s_r.at[j, way], at_x((xp, xm)[way]))

        def landed(j, way):
            blk = g.at[j, xrows((xm, xp)[way], r0, n), :]
            rc(blk, blk, s_s.at[j, way], s_r.at[j, way], at_x(xp)).wait_recv()

        def forward(j, way):
            blk = g.at[j, xrows((xm, xp)[way], r0 + way * h, h), :]
            return rc(blk, blk, f_s.at[j, way], f_r.at[j, way], at_x((xp, xm)[way]))

        def far_landed(j, way):
            blk = g.at[j, xrows(x2, r0 + way * h, h), :]
            rc(blk, blk, f_s.at[j, way], f_r.at[j, way], at_x(xp)).wait_recv()

        def pass_on(j):
            for way in range(2):
                landed(j, way)
                forward(j, way).start()

        return send, pass_on, forward, far_landed

    a_send, a_pass, a_fwd, a_far = ring(0, NA, a_s, a_r, af_s, af_r)
    b_send, b_pass, b_fwd, b_far = ring(NA, NB, b_s, b_r, bf_s, bf_r)

    @pl.loop(0, NC)
    def _(j):
        w_copy(j).wait()
        grads(j, 0, NA)
        a_send(j, 0).start()
        a_send(j, 1).start()

        @pl.when(j >= 2)
        def _():
            a_pass(j - 2)

        @pl.when(j == 2)
        def _():
            ob_landed(0)
            ob_step(3).start()
            ob_step(4).start()

        @pl.when(j == 4)
        def _():
            ob_landed(1)
            ob_landed(2)
            ob_step(5).start()
            ob_step(6).start()

        @pl.when(j == 5)
        def _():
            xg_landed(0)
            xg_step(3).start()
            xg_step(4).start()

        @pl.when(j == 7)
        def _():
            ob_landed(3)
            ob_landed(4)
            ob_step(7).start()
            ob_step(8).start()

        @pl.when(j == 9)
        def _():
            xg_landed(1)
            xg_landed(2)
            xg_step(5).start()
            xg_step(6).start()

    a_pass(NC - 2)
    a_pass(NC - 1)
    for i in range(5, 9):
        ob_landed(i)

    slots = ((1 - zl) * 2 + 1 - c, zl * 2 + 1 - c, (1 - zl) * 2 + c, zl * 2 + c)

    def build_xt():
        for i in range(5, 9):
            xg_landed(i)
        for s in range(4):
            cols = pl.ds(pl.multiple_of(slots[s] * 256, 256), 256)
            blk = xin[:, :, :, cols].reshape(T4, 256)
            xt[pl.ds(s * 256, 256), :] = blk.T
        for s in range(4):
            rows = xt[pl.ds(pl.multiple_of(s * 256 + t * 32, 32), 32), :]
            ic[pl.ds(s * 32, 32), :] = jnp.dot(
                rows, xin[...].reshape(T4, DB), preferred_element_type=F32
            )
        rc(ic.at[pl.ds(0, 64), :], icr, m_s.at[0], m_r.at[0], mate).start()

    def k_copy(j):
        return rc(
            ks.at[j % KSLOTS, pl.ds(0, 512), :], crv.at[j % KSLOTS], k_s.at[j], k_r.at[j], mate
        )

    def z_copy(j):
        return rc(zs.at[j], zr.at[j], z_s.at[j], z_r.at[j], across)

    def cov_copy(zz):
        rows = pl.ds(pl.multiple_of(64 * (x % 2) + (zz * 2 + 1 - c) * CR, 16), CR)
        return rc(cv.at[:, rows, :], ccr.at[zz], m_s.at[2 + zz], m_r.at[2 + zz], mate)

    zcov_copy = rc(zcs, zcr, m_s.at[4], m_r.at[4], across)

    def own_cov(zz, a):
        rows = pl.ds(pl.multiple_of(64 * (x % 2) + (zz * 2 + c) * CR, 16), CR)
        return cv[a, rows, :] + ccr[zz, a]

    def cov():
        b = x // 2
        for k in range(4):
            blk = g[BC * b + 3 * (x % 2) + k].T
            rt[0, pl.ds(k * CH, CH), :] = blk[:CH]
            rt[1, pl.ds(k * CH, CH), :] = blk[CH:]

        @pl.loop(0, BC)
        def _(k):
            cols = pl.ds(pl.multiple_of(k * CH, CH), CH)
            for a in range(2):
                cv[a, :, cols] = jnp.dot(
                    rt[a], g[BC * b + k, :, pl.ds(a * CH, CH)], preferred_element_type=F32
                )

        cov_copy(0).start()
        cov_copy(1).start()

    def cov_across():
        cov_copy(0).wait_recv()
        cov_copy(1).wait_recv()
        for a in range(2):
            zcs[a] = own_cov(1 - zl, a).astype(BF)
        zcov_copy.start()

    in_across = rc(zis, zir, m_s.at[1], m_r.at[1], across)

    @pl.loop(0, NC + 4)
    def _(j):
        @pl.when(j < NC)
        def _():
            grads(j, NA, NB)
            b_send(j, 0).start()
            b_send(j, 1).start()

        @pl.when(j == 0)
        def _():
            xg_landed(3)
            xg_landed(4)
            xg_step(7).start()
            xg_step(8).start()

        @pl.when(jnp.logical_and(j >= 1, j < NC + 1))
        def _():
            b_pass(j - 1)

        @pl.when(j == 2)
        def _():
            build_xt()

        @pl.when(jnp.logical_and(j >= 2, j < NC + 2))
        def _():
            i = j - 2
            for way in range(2):
                a_far(i, way)
                b_far(i, way)

            @pl.when(i >= KSLOTS)
            def _():
                k_copy(i - KSLOTS).wait_send()

            for m in range(4):
                ks[i % KSLOTS, pl.ds(m * 256, 256), :] = jnp.dot(
                    xt[pl.ds(m * 256, 256), :], g[i], preferred_element_type=F32
                )
            k_copy(i).start()

        @pl.when(jnp.logical_and(j >= 3, j < NC + 3))
        def _():
            i = j - 3
            k_copy(i).wait_recv()
            s = i % KSLOTS
            zs[i] = (ks[s, pl.ds(512, 256), :] + crv[s, pl.ds(0, 256), :]).astype(BF)
            z_copy(i).start()
            fin[i] = ks[s, pl.ds(768, 256), :] + crv[s, pl.ds(256, 256), :]

        @pl.when(j == 5)
        def _():
            rc(ic.at[pl.ds(0, 64), :], icr, m_s.at[0], m_r.at[0], mate).wait_recv()
            zis[...] = ic[pl.ds(64, 32), :] + icr[pl.ds(0, 32), :]
            in_across.start()

        @pl.when(jnp.logical_and(j == BC + 1, x < 2))
        def _():
            cov()

        @pl.when(jnp.logical_and(j == BC + 2, x < 2))
        def _():
            cov_across()

        @pl.when(jnp.logical_and(j == NC + 1, x >= 2))
        def _():
            cov()

        @pl.when(jnp.logical_and(j == NC + 2, x >= 2))
        def _():
            cov_across()

        @pl.when(j >= 4)
        def _():
            i = j - 4
            z_copy(i).wait_recv()
            tot = fin[i] + zr[i].astype(F32)
            hid = pl.ds(pl.multiple_of(i * CH, CH), CH)
            gw_ref[:, hid] = tot[:, :CH].astype(BF)
            uw_ref[:, hid] = tot[:, CH:].astype(BF)

    in_across.wait_recv()
    ic_ref[...] = (
        ic[pl.ds(96, 32), :] + icr[pl.ds(32, 32), :] + zir[...]
    ) * (1.0 / 4096.0)
    zcov_copy.wait_recv()
    gc_ref[...] = own_cov(zl, 0) + zcr[0].astype(F32)
    uc_ref[...] = own_cov(zl, 1) + zcr[1].astype(F32)

    for cp in oa:
        cp.wait_send()
    for i in range(9):
        ob_step(i).wait_send()
        xg_step(i).wait_send()
    for k in range(8):

        @pl.when(jnp.logical_not(jnp.logical_and(self_x, t == k)))
        def _():
            scatter(k).wait_send()

    @pl.loop(0, NC)
    def _(j):
        for way in range(2):
            a_send(j, way).wait_send()
            a_fwd(j, way).wait_send()
            b_send(j, way).wait_send()
            b_fwd(j, way).wait_send()
        z_copy(j).wait_send()

        @pl.when(j >= NC - KSLOTS)
        def _():
            k_copy(j).wait_send()

    rc(ic.at[pl.ds(0, 64), :], icr, m_s.at[0], m_r.at[0], mate).wait_send()
    in_across.wait_send()
    cov_copy(0).wait_send()
    cov_copy(1).wait_send()
    zcov_copy.wait_send()


def on_device(inputs, gate_pre, up_pre, out_grad, down_weight):
    dma = pltpu.SemaphoreType.DMA
    vm = pltpu.VMEM
    outs = pl.pallas_call(
        kernel,
        out_shape=(
            jax.ShapeDtypeStruct((TOK, H), BF),
            jax.ShapeDtypeStruct((TOK, H), BF),
            jax.ShapeDtypeStruct((32, DB), F32),
            jax.ShapeDtypeStruct((CR, HB), F32),
            jax.ShapeDtypeStruct((CR, HB), F32),
        ),
        in_specs=[pl.BlockSpec(memory_space=pl.ANY)] * 5,
        out_specs=tuple([pl.BlockSpec(memory_space=vm)] * 5),
        scratch_shapes=[
            vm((TOK, D), BF),
            vm((H, D), BF),
            vm((TOK, H), BF),
            vm((TOK, H), BF),
            vm((NC, T4, CW), BF),
            vm((4, 8, 32, DB), BF),
            vm((DB, T4), BF),
            vm((KSLOTS, DB, CW), F32),
            vm((KSLOTS, 512, CW), F32),
            vm((NC, TOK, CW), F32),
            vm((NC, TOK, CW), BF),
            vm((NC, TOK, CW), BF),
            vm((2, 512, T4), BF),
            vm((2, 512, HB), F32),
            vm((2, 2, CR, HB), F32),
            vm((2, CR, HB), BF),
            vm((2, CR, HB), BF),
            vm((128, DB), F32),
            vm((64, DB), F32),
            vm((32, DB), F32),
            vm((32, DB), F32),
            dma((3,)),
            dma((NC,)),
            dma((2, 4)), dma((2, 4)),
            dma((9,)), dma((9,)),
            dma((8,)), dma((8,)),
            dma((9,)), dma((9,)),
            dma((NC, 2)), dma((NC, 2)), dma((NC, 2)), dma((NC, 2)),
            dma((NC, 2)), dma((NC, 2)), dma((NC, 2)), dma((NC, 2)),
            dma((NC,)), dma((NC,)),
            dma((NC,)), dma((NC,)),
            dma((5,)), dma((5,)),
        ],
        compiler_params=pltpu.CompilerParams(
            collective_id=0, has_side_effects=True, vmem_limit_bytes=62 << 20
        ),
    )(inputs, gate_pre, up_pre, out_grad, down_weight)
    gw, uw, ic, gc, uc = outs
    return gw, uw, ic, gc[None], uc[None]


def solution(mesh):
    placed = (
        P("dp", "tensor"),
        P("dp", "tensor"),
        P("dp", "tensor"),
        P("dp", "tensor"),
        P("tensor", None),
    )
    return jax.shard_map(
        on_device,
        mesh=mesh,
        in_specs=placed,
        out_specs=(
            P("dp", "tensor"),
            P("dp", "tensor"),
            P(("dp", "tensor"), None),
            P("tensor", "dp", None),
            P("tensor", "dp", None),
        ),
        check_vma=False,
    )
```

```python
import jax
import jax.numpy as jnp
from jax import lax
from jax.experimental import pallas as pl
from jax.experimental.pallas import tpu as pltpu
from jax.sharding import PartitionSpec as P

MESH = pl.DeviceIdType.MESH
BF = jnp.bfloat16
F32 = jnp.float32

TOK = 256
NA = 64
NB = TOK - NA
D = 4096
DS = 512
H = 1792
CH = 128
CW = 2 * CH
NC = H // CH
BC = 7
HB = 896
T4 = 4 * TOK
DB = 1024
CR = 112
KSLOTS = 4
X0 = 4
ZLAG = 9


def kernel(
    x_hbm, gp_hbm, up_hbm, og_hbm, w_hbm,
    gw_hbm, uw_hbm, ic_hbm, gc_hbm, uc_hbm,
    og, w, gp, up, g, xs, xin, xt, ks, crv, fin, zs, zr, rt, cv, ccr, zcs, zcr, ic, icr, zis, zir, out,
    loc, wsem, osem,
    oa_s, oa_r, ob_s, ob_r, xs_s, xs_r, x2_s, x2_r, xg_s, xg_r,
    a_s, a_r, af_s, af_r, b_s, b_r, bf_s, bf_r,
    k_s, k_r, z_s, z_r, m_s, m_r,
):
    dp = lax.axis_index("dp")
    t = lax.axis_index("tensor")
    x, zl, c = dp // 4, (dp // 2) % 2, dp % 2
    zh, y = t // 4, t % 4
    xp, xm, x2 = (x + 1) % 4, (x + 3) % 4, (x + 2) % 4
    yp, ym, y2 = (y + 1) % 4, (y + 3) % 4, (y + 2) % 4
    inplane = zl * 2 + c

    def at_x(v):
        return (v * 4 + inplane, t)

    def at_t(zz, yy):
        return (dp, zz * 4 + yy)

    mate = (dp + 1 - 2 * c, t)
    across = (dp + 2 - 4 * zl, t)
    zo = 1 - zh
    peers = [(dz, dy) for dz in range(2) for dy in range(4) if (dz, dy) != (0, 0)]

    def to_peer(dz, dy):
        return (zh + dz) % 2, (y + dy) % 4

    def from_peer(dz, dy):
        return ((zh + 2 - dz) % 2) * 4 + (y + 4 - dy) % 4

    def rc(src, dst, ss, rs, dev):
        return pltpu.make_async_remote_copy(
            src_ref=src, dst_ref=dst, send_sem=ss, recv_sem=rs, device_id=dev, device_id_type=MESH
        )

    l_gp = pltpu.make_async_copy(gp_hbm, gp, loc.at[0])
    l_up = pltpu.make_async_copy(up_hbm, up, loc.at[1])
    own_cols = pl.ds(pl.multiple_of(t * DS, DS), DS)
    l_og = pltpu.make_async_copy(og_hbm, og.at[:, own_cols], loc.at[2])
    l_xs = pltpu.make_async_copy(
        x_hbm.at[pl.ds(pl.multiple_of(t * 32, 32), 32), :], xs.at[t], loc.at[3]
    )
    l_og.start()
    l_xs.start()
    l_gp.start()
    l_up.start()

    def w_copy(j):
        r = pl.ds(pl.multiple_of(j * CH, CH), CH)
        return pltpu.make_async_copy(w_hbm.at[r, :], w.at[r, :], wsem.at[j])

    @pl.loop(0, NC)
    def _(j):
        w_copy(j).start()

    barrier = pltpu.get_barrier_semaphore()
    greeted = [at_t(*to_peer(dz, dy)) for dz, dy in peers]
    greeted += [at_x(xp), at_x(xm), at_x(x2), mate, across]
    for dev in greeted:
        pl.semaphore_signal(barrier, inc=1, device_id=dev, device_id_type=MESH)
    pl.semaphore_wait(barrier, len(greeted))

    def oa_copy(dz, dy):
        return rc(
            og_hbm.at[pl.ds(0, NA), :],
            og.at[pl.ds(0, NA), own_cols],
            oa_s.at[dz, dy],
            oa_r.at[dz, dy],
            at_t(*to_peer(dz, dy)),
        )

    for dz, dy in peers:
        oa_copy(dz, dy).start()

    def spread(dz, dy):
        zz, yy = to_peer(dz, dy)
        rows = pl.ds(pl.multiple_of((zz * 4 + yy) * 32, 32), 32)
        return rc(
            x_hbm.at[rows, :], xs.at[t], xs_s.at[dz, dy], xs_r.at[dz, dy], at_t(zz, yy)
        )

    for dz, dy in peers:
        spread(dz, dy).start()

    def to_x(dx):
        v = (x + dx) % 4
        return rc(
            xs.at[pl.ds(2 * v, 2)], xin.at[:, x, t], x2_s.at[dx - 1], x2_r.at[dx - 1], at_x(v)
        )

    def all_to_x():
        l_xs.wait()
        for dz, dy in peers:
            dst = xs.at[from_peer(dz, dy)]
            rc(dst, dst, xs_s.at[dz, dy], xs_r.at[dz, dy], mate).wait_recv()
        for dx in (2, 1, 3):
            to_x(dx).start()
        pltpu.make_async_copy(xs.at[pl.ds(2 * x, 2)], xin.at[:, x, t], loc.at[4]).start()

    def from_x():
        pltpu.make_async_copy(xs.at[pl.ds(2 * x, 2)], xin.at[:, x, t], loc.at[4]).wait()
        for dx in (1, 2, 3):
            dst = xin.at[:, (x + 4 - dx) % 4, t]
            rc(dst, dst, x2_s.at[dx - 1], x2_r.at[dx - 1], mate).wait_recv()

    def og_part(owner, part):
        cols = pl.ds(pl.multiple_of(owner * DS, DS), DS)
        at, n = ((0, NB), (0, NB // 2), (NB // 2, NB // 2), (0, NB // 4), (NB // 4, NB // 4))[part]
        return og.at[pl.ds(NA + at, n), cols]

    def x_part(owner, part):
        at, n = ((0, 4), (0, 2), (2, 2), (0, 1), (1, 1))[part]
        return xin.at[:, pl.ds(at, n), owner]

    def gather(part_of, first, ss, rs):
        up1, dn1, zp = at_t(zh, yp), at_t(zh, ym), at_t(zo, y)
        out = (
            (t, 0, zp), (t, 0, up1), (t, 0, dn1),
            (zo * 4 + y, 1, up1), (zo * 4 + y, 1, dn1),
            (zh * 4 + ym, 1, up1), (zh * 4 + yp, 2, dn1),
            (zo * 4 + ym, 3, up1), (zo * 4 + yp, 4, dn1),
            (zh * 4 + ym, 2, zp), (zh * 4 + yp, 2, zp), (zh * 4 + y2, 2, zp),
        )
        come = (
            (zo * 4 + y, 0), (zh * 4 + ym, 0), (zh * 4 + yp, 0),
            (zo * 4 + ym, 1), (zo * 4 + yp, 1),
            (zh * 4 + y2, 1), (zh * 4 + y2, 2),
            (zo * 4 + y2, 3), (zo * 4 + y2, 4),
            (zo * 4 + ym, 2), (zo * 4 + yp, 2), (zo * 4 + y2, 2),
        )

        def step(i):
            owner, part, dev = out[i]
            dst = part_of(owner, part)
            return rc(first if i < 3 else dst, dst, ss.at[i], rs.at[i], dev)

        def landed(*which):
            for i in which:
                dst = part_of(*come[i])
                rc(dst, dst, ss.at[i], rs.at[i], zp).wait_recv()

        def go(*which):
            for i in which:
                step(i).start()

        return step, landed, go

    ob_step, ob_landed, ob_go = gather(og_part, og_hbm.at[pl.ds(NA, NB), :], ob_s, ob_r)
    xg_step, xg_landed, xg_go = gather(x_part, x_part(t, 0), xg_s, xg_r)
    ob_go(0, 1, 2)

    l_og.wait()
    l_gp.wait()
    l_up.wait()
    for dz, dy in peers:
        dst = og.at[pl.ds(0, NA), pl.ds(pl.multiple_of(from_peer(dz, dy) * DS, DS), DS)]
        rc(dst, dst, oa_s.at[dz, dy], oa_r.at[dz, dy], mate).wait_recv()

    def grads(j, r0, n):
        hid = pl.ds(pl.multiple_of(j * CH, CH), CH)
        hg = lax.dot_general(
            og[pl.ds(r0, n), :], w[hid, :], (((1,), (1,)), ((), ())), preferred_element_type=F32
        )
        gate = gp[pl.ds(r0, n), hid].astype(F32)
        upv = up[pl.ds(r0, n), hid].astype(F32)
        sig = jax.nn.sigmoid(gate)
        hs = hg * sig
        rows = pl.ds(pl.multiple_of(x * TOK + r0, 16), n)
        g[j, rows, pl.ds(0, CH)] = (hs * upv * (1.0 + gate * (1.0 - sig))).astype(BF)
        g[j, rows, pl.ds(CH, CH)] = (hs * gate).astype(BF)

    def xrows(xx, r0, n):
        return pl.ds(pl.multiple_of(xx * TOK + r0, 16), n)

    def ring(r0, n, s_s, s_r, f_s, f_r):
        h = n // 2

        def send(j, way):
            blk = g.at[j, xrows(x, r0, n), :]
            return rc(blk, blk, s_s.at[j, way], s_r.at[j, way], at_x((xp, xm)[way]))

        def landed(j, way):
            blk = g.at[j, xrows((xm, xp)[way], r0, n), :]
            rc(blk, blk, s_s.at[j, way], s_r.at[j, way], at_x(xp)).wait_recv()

        def forward(j, way):
            blk = g.at[j, xrows((xm, xp)[way], r0 + way * h, h), :]
            return rc(blk, blk, f_s.at[j, way], f_r.at[j, way], at_x((xp, xm)[way]))

        def far_landed(j, way):
            blk = g.at[j, xrows(x2, r0 + way * h, h), :]
            rc(blk, blk, f_s.at[j, way], f_r.at[j, way], at_x(xp)).wait_recv()

        def pass_on(j):
            for way in range(2):
                landed(j, way)
                forward(j, way).start()

        return send, pass_on, forward, far_landed

    a_send, a_pass, a_fwd, a_far = ring(0, NA, a_s, a_r, af_s, af_r)
    b_send, b_pass, b_fwd, b_far = ring(NA, NB, b_s, b_r, bf_s, bf_r)

    @pl.loop(0, NC)
    def _(j):
        w_copy(j).wait()
        grads(j, 0, NA)
        a_send(j, 0).start()
        a_send(j, 1).start()

        @pl.when(j >= 2)
        def _():
            a_pass(j - 2)

        @pl.when(j == 1)
        def _():
            all_to_x()

        @pl.when(j == 3)
        def _():
            ob_landed(0)
            ob_go(3, 4)

        @pl.when(j == 4)
        def _():
            ob_landed(1, 2)
            ob_go(5, 6, 9, 10)

        @pl.when(j == 6)
        def _():
            from_x()
            xg_go(0, 1, 2)

        @pl.when(j == 8)
        def _():
            ob_landed(3, 4)
            ob_go(7, 8)

        @pl.when(j == 9)
        def _():
            ob_landed(6)
            ob_go(11)

        @pl.when(j == 12)
        def _():
            xg_landed(0)
            xg_go(3, 4)

    a_pass(NC - 2)
    a_pass(NC - 1)
    ob_landed(5, 7, 8, 9, 10, 11)

    slots = ((1 - zl, 1 - c), (zl, 1 - c), (1 - zl, c), (zl, c))
    ic_copy = rc(ic.at[pl.ds(0, 64), :], icr, m_s.at[0], m_r.at[0], mate)
    in_across = rc(zis, zir, m_s.at[1], m_r.at[1], across)

    def build_xt():
        xg_landed(5, 7, 8, 9, 10, 11)
        for s in range(4):
            hi, lo = slots[s]
            cols = pl.ds(pl.multiple_of(lo * 256, 256), 256)
            xt[pl.ds(s * 256, 256), :] = xin[hi, :, :, :, cols].reshape(T4, 256).T

    def in_cov():
        rows = jnp.concatenate(
            [xt[pl.ds(pl.multiple_of(s * 256 + t * 32, 32), 32), :] for s in range(4)], axis=0
        )
        for h in range(2):
            ic[:, pl.ds(h * 512, 512)] = jnp.dot(
                rows, xin[h].reshape(T4, 512), preferred_element_type=F32
            )
        ic_copy.start()

    def k_copy(j):
        return rc(
            ks.at[j % KSLOTS, pl.ds(0, 512), :], crv.at[j % KSLOTS], k_s.at[j], k_r.at[j], mate
        )

    def z_copy(j):
        return rc(zs.at[j], zr.at[j], z_s.at[j], z_r.at[j], across)

    def cov_copy(zz):
        rows = pl.ds(pl.multiple_of(64 * (x % 2) + (zz * 2 + 1 - c) * CR, 16), CR)
        return rc(cv.at[:, rows, :], ccr.at[zz], m_s.at[2 + zz], m_r.at[2 + zz], mate)

    zcov_copy = rc(zcs, zcr, m_s.at[4], m_r.at[4], across)

    def own_cov(zz, a):
        rows = pl.ds(pl.multiple_of(64 * (x % 2) + (zz * 2 + c) * CR, 16), CR)
        return cv[a, rows, :] + ccr[zz, a]

    def cov():
        b = x // 2
        for k in range(4):
            blk = g[BC * b + 3 * (x % 2) + k].T
            rt[0, pl.ds(k * CH, CH), :] = blk[:CH]
            rt[1, pl.ds(k * CH, CH), :] = blk[CH:]

        for a in range(2):
            half = pl.ds(a * CH, CH)

            @pl.loop(0, 3)
            def _(k):
                two = jnp.concatenate(
                    [g[BC * b + 2 * k, :, half], g[BC * b + 2 * k + 1, :, half]], axis=1
                )
                cv[a, :, pl.ds(pl.multiple_of(k * CW, CW), CW)] = jnp.dot(
                    rt[a], two, preferred_element_type=F32
                )

            cv[a, :, pl.ds(6 * CH, CH)] = jnp.dot(
                rt[a], g[BC * b + 6, :, half], preferred_element_type=F32
            )
        cov_copy(0).start()
        cov_copy(1).start()

    def cov_across():
        cov_copy(0).wait_recv()
        cov_copy(1).wait_recv()
        for a in range(2):
            zcs[a] = own_cov(1 - zl, a).astype(BF)
        zcov_copy.start()

    def weigh(i):
        for way in range(2):
            a_far(i, way)
            b_far(i, way)

        @pl.when(i >= KSLOTS)
        def _():
            k_copy(i - KSLOTS).wait_send()

        for m in range(4):
            ks[i % KSLOTS, pl.ds(m * 256, 256), :] = jnp.dot(
                xt[pl.ds(m * 256, 256), :], g[i], preferred_element_type=F32
            )
        k_copy(i).start()

    def combine(i):
        k_copy(i).wait_recv()
        s = i % KSLOTS
        zs[i] = (ks[s, pl.ds(512, 256), :] + crv[s, pl.ds(0, 256), :]).astype(BF)
        z_copy(i).start()
        fin[i] = ks[s, pl.ds(768, 256), :] + crv[s, pl.ds(256, 256), :]

    def out_copy(i, a):
        hid = pl.ds(pl.multiple_of(i * CH, CH), CH)
        return pltpu.make_async_copy(
            out.at[a, :, hid], (gw_hbm, uw_hbm)[a].at[:, hid], osem.at[i, a]
        )

    def finish(i):
        z_copy(i).wait_recv()
        tot = fin[i] + zr[i].astype(F32)
        hid = pl.ds(pl.multiple_of(i * CH, CH), CH)
        out[0, :, hid] = tot[:, :CH].astype(BF)
        out[1, :, hid] = tot[:, CH:].astype(BF)
        out_copy(i, 0).start()
        out_copy(i, 1).start()

    def weighed(j):
        return jnp.where(j < X0, 0, jnp.minimum(jnp.minimum(2 * (j - X0 + 1), j - 1), NC))

    @pl.loop(0, NC + 3)
    def _(j):
        @pl.when(j < NC)
        def _():
            grads(j, NA, NB)
            b_send(j, 0).start()
            b_send(j, 1).start()

        @pl.when(j == 0)
        def _():
            xg_landed(1, 2)
            xg_go(5, 6, 9, 10)

        @pl.when(jnp.logical_and(j >= 1, j < NC + 1))
        def _():
            b_pass(j - 1)

        @pl.when(j == 1)
        def _():
            xg_landed(3, 4)
            xg_go(7, 8)
            xg_landed(6)
            xg_go(11)

        @pl.when(j == X0 - 1)
        def _():
            build_xt()

        @pl.when(j == X0 + 3)
        def _():
            in_cov()

        @pl.when(j == X0 + 4)
        def _():
            ic_copy.wait_recv()
            zis[...] = ic[pl.ds(64, 32), :] + icr[pl.ds(0, 32), :]
            in_across.start()

        @pl.loop(weighed(j - 2), weighed(j - 1))
        def _(i):
            combine(i)

        @pl.loop(weighed(j - 1), weighed(j))
        def _(i):
            weigh(i)

        @pl.when(jnp.logical_and(j == BC + 2, x < 2))
        def _():
            cov()

        @pl.when(jnp.logical_and(j == BC + 3, x < 2))
        def _():
            cov_across()

        @pl.when(jnp.logical_and(j == NC + 1, x >= 2))
        def _():
            cov()

        @pl.when(jnp.logical_and(j == NC + 2, x >= 2))
        def _():
            cov_across()

        @pl.when(j >= ZLAG)
        def _():
            finish(j - ZLAG)

    in_across.wait()
    zis[...] = (ic[pl.ds(96, 32), :] + icr[pl.ds(32, 32), :] + zir[...]) * (1.0 / 4096.0)

    @pl.loop(NC + 3 - ZLAG, NC)
    def _(i):
        finish(i)

    zcov_copy.wait_recv()
    for a in range(2):
        ccr[zl, a] = own_cov(zl, a) + zcr[a].astype(F32)
    last = [
        pltpu.make_async_copy(zis, ic_hbm, loc.at[0]),
        pltpu.make_async_copy(ccr.at[zl, 0], gc_hbm, loc.at[1]),
        pltpu.make_async_copy(ccr.at[zl, 1], uc_hbm, loc.at[2]),
    ]
    for cp in last:
        cp.start()

    for dz, dy in peers:
        oa_copy(dz, dy).wait_send()
        spread(dz, dy).wait_send()
    for dx in (1, 2, 3):
        to_x(dx).wait_send()
    for i in range(12):
        ob_step(i).wait_send()
        xg_step(i).wait_send()

    @pl.loop(0, NC)
    def _(j):
        for way in range(2):
            a_send(j, way).wait_send()
            a_fwd(j, way).wait_send()
            b_send(j, way).wait_send()
            b_fwd(j, way).wait_send()
            out_copy(j, way).wait()
        z_copy(j).wait_send()

        @pl.when(j >= NC - KSLOTS)
        def _():
            k_copy(j).wait_send()

    ic_copy.wait_send()
    cov_copy(0).wait_send()
    cov_copy(1).wait_send()
    zcov_copy.wait_send()
    for cp in last:
        cp.wait()


def copy_all(*refs):
    ins, outs, held, sems = refs[:5], refs[5:10], refs[10:15], refs[15]
    first = [pltpu.make_async_copy(ins[i], held[i], sems.at[0, i]) for i in range(5)]
    then = [pltpu.make_async_copy(held[i], outs[i], sems.at[1, i]) for i in range(5)]
    for cp in first:
        cp.start()
    for a, b in zip(first, then):
        a.wait()
        b.start()
    for cp in then:
        cp.wait()


def on_device(inputs, gate_pre, up_pre, out_grad, down_weight):
    dma = pltpu.SemaphoreType.DMA
    vm = pltpu.VMEM
    shapes = (
        jax.ShapeDtypeStruct((TOK, H), BF),
        jax.ShapeDtypeStruct((TOK, H), BF),
        jax.ShapeDtypeStruct((32, DB), F32),
        jax.ShapeDtypeStruct((CR, HB), F32),
        jax.ShapeDtypeStruct((CR, HB), F32),
    )
    anywhere = pl.BlockSpec(memory_space=pl.ANY)
    outs = pl.pallas_call(
        kernel,
        out_shape=shapes,
        in_specs=[anywhere] * 5,
        out_specs=tuple([anywhere] * 5),
        scratch_shapes=[
            vm((TOK, D), BF),
            vm((H, D), BF),
            vm((TOK, H), BF),
            vm((TOK, H), BF),
            vm((NC, T4, CW), BF),
            vm((8, 32, DS), BF),
            vm((2, 4, 8, 32, DS), BF),
            vm((DB, T4), BF),
            vm((KSLOTS, DB, CW), F32),
            vm((KSLOTS, 512, CW), F32),
            vm((NC, TOK, CW), F32),
            vm((NC, TOK, CW), BF),
            vm((NC, TOK, CW), BF),
            vm((2, 512, T4), BF),
            vm((2, 512, HB), F32),
            vm((2, 2, CR, HB), F32),
            vm((2, CR, HB), BF),
            vm((2, CR, HB), BF),
            vm((128, DB), F32),
            vm((64, DB), F32),
            vm((32, DB), F32),
            vm((32, DB), F32),
            vm((2, TOK, H), BF),
            dma((5,)),
            dma((NC,)),
            dma((NC, 2)),
            dma((2, 4)), dma((2, 4)),
            dma((12,)), dma((12,)),
            dma((2, 4)), dma((2, 4)),
            dma((3,)), dma((3,)),
            dma((12,)), dma((12,)),
            dma((NC, 2)), dma((NC, 2)), dma((NC, 2)), dma((NC, 2)),
            dma((NC, 2)), dma((NC, 2)), dma((NC, 2)), dma((NC, 2)),
            dma((NC,)), dma((NC,)),
            dma((NC,)), dma((NC,)),
            dma((5,)), dma((5,)),
        ],
        compiler_params=pltpu.CompilerParams(
            collective_id=0, has_side_effects=True, vmem_limit_bytes=62 << 20
        ),
    )(inputs, gate_pre, up_pre, out_grad, down_weight)
    gw, uw, ic, gc, uc = pl.pallas_call(
        copy_all,
        out_shape=shapes,
        in_specs=[anywhere] * 5,
        out_specs=tuple([anywhere] * 5),
        scratch_shapes=[vm(a.shape, a.dtype) for a in shapes] + [dma((2, 5))],
    )(*outs)
    return gw, uw, ic, gc[None], uc[None]


def solution(mesh):
    placed = (
        P("dp", "tensor"),
        P("dp", "tensor"),
        P("dp", "tensor"),
        P("dp", "tensor"),
        P("tensor", None),
    )
    return jax.shard_map(
        on_device,
        mesh=mesh,
        in_specs=placed,
        out_specs=(
            P("dp", "tensor"),
            P("dp", "tensor"),
            P(("dp", "tensor"), None),
            P("tensor", "dp", None),
            P("tensor", "dp", None),
        ),
        check_vma=False,
    )
```
